512 devices in a mesh: pair: 64 (over x, z, core), win: 8 (over y).
Axes of the slice: x: 4, y: 8, z: 8, core: 2. Of those that a mesh axis runs over, the one named last changes fastest.
Arguments:
- windows: bfloat16 [8, 2048, 8192], P('win', None, 'pair'), may hold values from -4 to 4
- pair_offset: int32 [64, 4], P('pair'), may hold values from 1 to 4, as said below
- pair_count: int32 [64], P('pair'), may hold values from 0 to 4, as said below
- pair_mask: int32 [256, 128], P('pair'), may hold values 0 or 1
Outputs:
- stacks: float32 [512, 256, 128], P('win', 'pair')
The draws below stay inside these ranges and needn't reach their ends.
Inputs may be any that keep to these rules, and one draw needn't show every extreme that they name: Row d holds the numbers 1 to 4, each once; slots from pair_count[d] on are empty; every live slot's partner block d + pair_offset[d, s] is below 64; for d >= 60 the row is 1, 2, ... in order. `pair_count`: block d >= 60 owns 64 - 1 - d live pair blocks; block 59 owns 4.
All inputs are finite; a program needn't handle non-finite values. No bound on the sum of `pair_mask` on one device may be relied on, other than what follows from the above.
Results may differ from the reference program's by a relative error of at most 0.01.
Values may be sent and summed in bfloat16 or wider, within the bound.
A program may use at most 64 MiB of HBM per device.

```python
import math
import jax
import jax.numpy as jnp
from jax import lax

L = 2048
CH = 128
FB = 512
F0 = 64
LAGS = 512
REACH = 4
WINDOWS = 8
NBLK = 64
CHANNELS = 8192
PAIRS = 256


def pair_layout(key):
    score_key = jax.random.fold_in(key, 101)
    count_key = jax.random.fold_in(key, 202)
    scores = jax.random.randint(score_key, (NBLK, REACH), 0, 65536) * REACH + jnp.arange(REACH, dtype=jnp.int32)[None, :]
    offsets = jnp.argsort(scores, axis=1, stable=True).astype(jnp.int32) + 1
    counts = jax.random.randint(count_key, (NBLK,), 1, REACH + 1)
    blocks = jnp.arange(NBLK, dtype=jnp.int32)
    tail = blocks >= NBLK - REACH
    ordered = jnp.arange(REACH, dtype=jnp.int32)[None, :] + 1
    offsets = jnp.where(tail[:, None], ordered, offsets)
    counts = jnp.where(blocks == NBLK - 1 - REACH, REACH, counts)
    counts = jnp.where(tail, NBLK - 1 - blocks, counts)
    return (offsets.astype(jnp.int32), counts.astype(jnp.int32))


def draw_pair_offset(key, part):
    return pair_layout(key)[0]


def draw_pair_count(key, part):
    return pair_layout(key)[1]


def draw_windows(key, part):
    delay_key = jax.random.fold_in(key, 301)
    lower_key = jax.random.fold_in(key, 302)
    upper_key = jax.random.fold_in(key, 303)
    angle_key = jax.random.fold_in(key, 304)
    source_key = jax.random.fold_in(key, 305)
    white_key = jax.random.fold_in(key, 306)
    max_delay = LAGS // 2 + LAGS // 8
    odd_blocks = (jnp.arange(NBLK, dtype=jnp.int32) % 2).astype(jnp.int32)
    delays = odd_blocks * jax.random.randint(delay_key, (NBLK,), LAGS // 2 - LAGS // 16, max_delay)
    samples = jnp.arange(L, dtype=jnp.int32)
    source_rows = samples[:, None] + max_delay - delays[None, :]
    lower_bin = jax.random.randint(lower_key, (WINDOWS,), F0 - 8, F0 - 2)
    upper_bin = jax.random.randint(upper_key, (WINDOWS,), F0 + FB + 2, F0 + FB + 8)
    lower_phase = (lower_bin[:, None] * samples[None, :] % (2 * L)).astype(jnp.float32) * (math.pi / L)
    upper_phase = (upper_bin[:, None] * samples[None, :] % (2 * L)).astype(jnp.float32) * (math.pi / L)
    angles = jax.random.uniform(angle_key, (2, WINDOWS, 1, CH), jnp.float32, -math.pi, math.pi)
    shape = (WINDOWS, L, NBLK, CH)
    white_noise = 0.7 * jax.random.normal(white_key, shape, jnp.float32)
    tone_scale = 0.8
    source_scale = 0.25
    tone_field = tone_scale * (jnp.cos(lower_phase[:, :, None] + angles[0]) + jnp.cos(upper_phase[:, :, None] + angles[1]))
    source = source_scale * jax.random.normal(source_key, (WINDOWS, L + max_delay, CH), jnp.float32)
    delayed = source[:, source_rows, :]
    combined = white_noise + delayed + tone_field[:, :, None, :]
    combined = jnp.clip(combined, -4.0, 4.0)
    return combined.reshape(WINDOWS, L, CHANNELS).astype(jnp.bfloat16)


def touch_ends(result, stream_key, least, largest):
    extent = result.shape
    place = [jax.random.randint(jax.random.fold_in(stream_key, axis), (), 0, extent[axis]) for axis in range(len(extent))]
    result = result.at[tuple(place)].set(least)
    longest = extent.index(max(extent))
    place[longest] = (place[longest] + 1) % extent[longest]
    return result.at[tuple(place)].set(largest)


def setup_inputs(seed: int = 0) -> dict:
    seeds = jax.random.split(jax.random.key(seed), 5)
    windows = draw_windows(jax.random.fold_in(seeds[4], 71), 0)
    pair_offset = draw_pair_offset(jax.random.fold_in(seeds[4], 71), 0)
    pair_count = draw_pair_count(jax.random.fold_in(seeds[4], 71), 0)
    pair_mask = touch_ends((jax.random.randint(seeds[3], (PAIRS, CH), 0, 4) < 3).astype(jnp.int32), jax.random.fold_in(seeds[3], 1), 0, 1)
    return {"windows": windows, "pair_offset": pair_offset, "pair_count": pair_count, "pair_mask": pair_mask}


def reference(windows, pair_offset, pair_count, pair_mask):
    frame_total, length, channel_total = windows.shape
    block_total, reach_total = pair_offset.shape
    block_width = pair_mask.shape[1]
    nfft = 2 * length
    owners = jnp.arange(block_total, dtype=jnp.int32)[:, None]
    partner = jnp.clip(owners + pair_offset, 0, block_total - 1).astype(jnp.int32)
    live_slots = (jnp.arange(reach_total, dtype=jnp.int32)[None, :] < pair_count[:, None]).astype(jnp.float32)
    weight = live_slots[:, :, None] * pair_mask.reshape(block_total, reach_total, block_width).astype(jnp.float32)

    def accumulate(totals, window_now):
        padded = jnp.concatenate([window_now.astype(jnp.float32), jnp.zeros((length, channel_total), jnp.float32)], axis=0)
        spectra = jnp.fft.fft(padded, axis=0)[F0:F0 + FB]
        real_low = jnp.real(spectra).astype(jnp.float32).astype(jnp.bfloat16)
        imag_low = jnp.imag(spectra).astype(jnp.float32).astype(jnp.bfloat16)
        real_low, imag_low = lax.optimization_barrier((real_low, imag_low))
        real_part = real_low.astype(jnp.float32).reshape(FB, block_total, block_width)
        imag_part = imag_low.astype(jnp.float32).reshape(FB, block_total, block_width)
        own_real = real_part[:, :, None, :]
        own_imag = imag_part[:, :, None, :]
        other_real = real_part[:, partner, :]
        other_imag = imag_part[:, partner, :]
        real_sum = own_real * other_real + own_imag * other_imag
        imag_sum = own_imag * other_real - own_real * other_imag
        return ((totals[0] + real_sum, totals[1] + imag_sum), None)
    zero_sums = jnp.zeros((FB, block_total, reach_total, block_width), jnp.float32)
    (real_total, imag_total), _ = lax.scan(accumulate, (zero_sums, zero_sums), windows)
    real_total = (real_total * weight[None]).reshape(FB, -1)
    imag_total = (imag_total * weight[None]).reshape(FB, -1)
    lag_values = jnp.arange(LAGS, dtype=jnp.int32) - LAGS // 2
    frequency = F0 + jnp.arange(FB, dtype=jnp.int32)
    phases = (lag_values[:, None] * frequency[None, :] % nfft).astype(jnp.float32) * (2.0 * math.pi / nfft)
    factor = 1.0 / (length * math.sqrt(FB * frame_total))
    stacks = jnp.dot(jnp.cos(phases), real_total, precision=lax.Precision.HIGHEST) - jnp.dot(jnp.sin(phases), imag_total, precision=lax.Precision.HIGHEST)
    return (stacks * factor).reshape(LAGS, block_total * reach_total, block_width)
```

```python
import functools
import math

import jax
import jax.numpy as jnp
import numpy as np
from jax import lax
from jax.experimental import pallas as pl
from jax.experimental.pallas import tpu as pltpu
from jax.sharding import PartitionSpec as P

FB = 512
F0 = 64
LAGS = 512
LENGTH = 2048
CH = 128
SPLIT = 4
FOLD = LENGTH // SPLIT
QUARTERS = 4
HALVES = 2
ROWS = 8
SEND = jnp.bfloat16
MESH = pl.DeviceIdType.MESH
PAIRS = ((2, 3), (2, 4), (2, 5), (3, 4), (3, 5), (0, 4), (1, 4), (1, 5))
TILES = ((0, 1), (2, 2), (3, 4), (5, 5), (6, 7))


def quarter_bins(quarter):
    steps = 8 * np.arange(FB // 8)
    return np.concatenate([steps + 2 * quarter, steps + 2 * quarter + 1])


def two_parts(table):
    high = table.astype(jnp.bfloat16)
    rest = (table - high.astype(np.float64)).astype(jnp.bfloat16)
    return high, rest


def forward_table():
    nfft = 2 * LENGTH
    parts = []
    for quarter in range(QUARTERS):
        phase = 2 * np.pi * ((F0 + quarter_bins(quarter))[:, None] * np.arange(FOLD)[None, :] % nfft) / nfft
        table = np.concatenate([np.cos(phase), -np.sin(phase)], axis=0)
        parts.append(np.concatenate(two_parts(table), axis=1))
    return np.stack(parts)


def lag_turns():
    bins = np.concatenate([quarter_bins(quarter) for quarter in range(QUARTERS)])
    phase = 2 * np.pi * ((F0 + bins) * (LAGS // 2) % (2 * LENGTH)) / (2 * LENGTH)
    return np.stack([np.cos(phase), np.sin(phase)]).astype(np.float32)


def weighted(terms):
    total = None
    for weight, value in terms:
        if abs(weight) < 1e-9:
            continue
        if abs(abs(weight) - 1.0) > 1e-9:
            value = value * np.float32(abs(weight))
        if total is None:
            total = value if weight > 0 else -value
        else:
            total = total + value if weight > 0 else total - value
    return total


def kernel(
    chips, wins, factor, x_hbm, fwd_hbm, turn_ref, off_ref, cnt_ref, mask_ref, out_ref,
    xbuf, fwd, spec, gath, acc, res, fin,
    load_sem, a_send, a_recv, z_send, z_recv, f_send, f_recv,
):
    pair, win = lax.axis_index("pair"), lax.axis_index("win")
    chip, core = pair // 2, pair % 2
    before, after = (chip + chips - 1) % chips, (chip + 1) % chips
    group = win * 2 + core
    groups = 2 * wins

    x_copy = pltpu.make_async_copy(x_hbm.at[0], xbuf, load_sem.at[0])
    x_copy.start()
    fwd_copies = []
    for quarter in range(QUARTERS):
        copy = pltpu.make_async_copy(fwd_hbm.at[quarter], fwd.at[quarter], load_sem.at[1 + quarter])
        copy.start()
        fwd_copies.append(copy)

    barrier = pltpu.get_barrier_semaphore()

    def greet(step, carry):
        there, side = (win + step // 2) % wins, (core + step % 2) % 2

        @pl.when(step > 0)
        def _():
            pl.semaphore_signal(barrier, inc=1, device_id=(2 * chip + side, there), device_id_type=MESH)

        pl.semaphore_signal(barrier, inc=1, device_id=(2 * after + side, there), device_id_type=MESH)
        return carry

    lax.fori_loop(0, groups, greet, 0)
    pl.semaphore_signal(barrier, inc=1, device_id=(2 * before + core, win), device_id_type=MESH)

    acc[...] = jnp.zeros_like(acc)

    def near(step):
        turn = (step % 2) * ((step + 1) // 2) + (1 - step % 2) * (wins - step // 2)
        return (win + turn) % wins

    def exchange(half, there, side):
        return pltpu.make_async_remote_copy(
            src_ref=spec.at[half, there * 2 + side],
            dst_ref=gath.at[1, win, core, half],
            send_sem=a_send.at[half, there, side],
            recv_sem=a_recv.at[half, win, core],
            device_id=(2 * chip + side, there),
            device_id_type=MESH,
        )

    def arrival(half, there, side):
        return pltpu.make_async_remote_copy(
            src_ref=spec.at[half, there * 2 + side],
            dst_ref=gath.at[1, there, side, half],
            send_sem=a_send.at[half, there, side],
            recv_sem=a_recv.at[half, there, side],
            device_id=(2 * chip + side, there),
            device_id_type=MESH,
        )

    x_copy.wait()
    for half in range(HALVES):
        for part in range(QUARTERS // HALVES):
            quarter = half * (QUARTERS // HALVES) + part
            fwd_copies[quarter].wait()
            wide = jnp.concatenate([xbuf[h * FOLD:(h + 1) * FOLD, :] for h in range(SPLIT)], axis=1)
            whole = jnp.dot(fwd[quarter, :, :FOLD], wide, preferred_element_type=jnp.float32)
            whole += jnp.dot(fwd[quarter, :, FOLD:], wide, preferred_element_type=jnp.float32)
            reals, imags = [], []
            for odd in range(2):
                residue = 2 * quarter + odd
                real_terms, imag_terms = [], []
                for h in range(SPLIT):
                    turn = 2 * math.pi * ((residue * h) % 8) / 8
                    real = whole[odd * 64:odd * 64 + 64, h * CH:(h + 1) * CH]
                    imag = whole[128 + odd * 64:128 + odd * 64 + 64, h * CH:(h + 1) * CH]
                    real_terms += [(math.cos(turn), real), (math.sin(turn), imag)]
                    imag_terms += [(math.cos(turn), imag), (-math.sin(turn), real)]
                reals.append(weighted(real_terms))
                imags.append(weighted(imag_terms))
            for kind, value in enumerate((reals, imags)):
                turned = jnp.concatenate(value, axis=0).T.reshape(groups, ROWS, 128)
                lane = part * 256 + kind * 128
                spec[half, :, :, lane:lane + 128] = turned.astype(jnp.bfloat16)
        if half == 0:
            pl.semaphore_wait(barrier, 2 * groups)

        def send(step, carry, half=half):
            there, side = near(step // 2), (core + step % 2) % 2
            exchange(half, there, side).start()
            return carry

        lax.fori_loop(1, groups, send, 0)
        gath[1, win, core, half] = spec[half, group]

    def forward(there, up):
        return pltpu.make_async_remote_copy(
            src_ref=gath.at[1, there],
            dst_ref=gath.at[0 if up else 2, there],
            send_sem=z_send.at[1 if up else 0, there],
            recv_sem=z_recv.at[0 if up else 1, there],
            device_id=(2 * (after if up else before) + core, win),
            device_id_type=MESH,
        )

    def multiply(there):
        for quarter in range(QUARTERS):
            half, lane = quarter // (QUARTERS // HALVES), quarter % (QUARTERS // HALVES) * 256
            blocks = []
            for block in range(6):
                both = gath[block // 2, there, block % 2, half, :, lane:lane + 256].astype(jnp.float32)
                blocks.append((both[:, :128], both[:, 128:]))
            for index, (own, other) in enumerate(PAIRS):
                (own_real, own_imag), (other_real, other_imag) = blocks[own], blocks[other]
                rows = slice(index * ROWS, index * ROWS + ROWS)
                left = slice(quarter * 256, quarter * 256 + 128)
                right = slice(quarter * 256 + 128, quarter * 256 + 256)
                acc[rows, left] += own_real * other_real + own_imag * other_imag
                acc[rows, right] += own_imag * other_real - own_real * other_imag

    lag = 3

    def travel(step, carry):
        @pl.when(step < wins)
        def _():
            there = near(step)
            for half in range(HALVES):
                arrival(half, there, 1 - core).wait_recv()

                @pl.when(step > 0)
                def _():
                    arrival(half, there, core).wait_recv()
            forward(there, True).start()
            forward(there, False).start()

        @pl.when(step >= lag)
        def _():
            there = near(step - lag)
            forward(there, True).wait_recv()
            forward(there, False).wait_recv()
            multiply(there)
        return carry

    lax.fori_loop(0, wins + lag, travel, 0)

    count = len(PAIRS) * ROWS
    stacks = jnp.zeros((count, LAGS), jnp.float32)
    for quarter in range(QUARTERS):
        bins = slice(quarter * 128, quarter * 128 + 128)
        cosine, sine = turn_ref[0:1, bins] * factor, turn_ref[1:2, bins] * factor
        real = acc[:, quarter * 256:quarter * 256 + 128]
        imag = acc[:, quarter * 256 + 128:quarter * 256 + 256]
        cross = jnp.concatenate([real * cosine + imag * sine, imag * cosine - real * sine], axis=1)
        high = cross.astype(jnp.bfloat16)
        rest = (cross - high.astype(jnp.float32)).astype(jnp.bfloat16)
        both = jnp.concatenate([high, rest], axis=0)
        upper = jnp.dot(both, fwd[quarter, :, :FOLD], preferred_element_type=jnp.float32)
        stacks += upper[:count] + upper[count:]
        stacks += jnp.dot(high, fwd[quarter, :, FOLD:], preferred_element_type=jnp.float32)
    lanes = lax.broadcasted_iota(jnp.int32, (ROWS, 128), 1)
    for column in range(LAGS // 128):
        for tile, (left, right) in enumerate(TILES):
            a = stacks[left * ROWS:(left + 1) * ROWS, column * 128:(column + 1) * 128]
            b = stacks[right * ROWS:(right + 1) * ROWS, column * 128:(column + 1) * 128]
            even = jnp.where(lanes < 64, a, pltpu.roll(b, 64, 1))
            odd = jnp.where(lanes < 64, pltpu.roll(a, 64, 1), b)
            res[2 * column, tile] = even.astype(SEND)
            res[2 * column + 1, tile] = odd.astype(SEND)

    def deliver(there, kind):
        first, size, slot = ((0, 2, 0), (2, 1, 0), (3, 1, 2), (4, 1, 2))[kind]
        where = chip if kind < 2 else before
        return pltpu.make_async_remote_copy(
            src_ref=res.at[there, first:first + size],
            dst_ref=fin.at[group, slot:slot + size],
            send_sem=f_send.at[kind, there],
            recv_sem=f_recv.at[0 if kind < 2 else 1],
            device_id=(2 * where + kind % 2, there),
            device_id_type=MESH,
        )

    def hand_out(step, carry):
        there = (win + step) % wins
        for kind in (2, 3, 0, 1):
            if kind < 2:
                @pl.when((step > 0) | (core != kind))
                def _():
                    deliver(there, kind).start()
            else:
                deliver(there, kind).start()
        return carry

    lax.fori_loop(0, wins, hand_out, 0)

    @pl.when(core == 0)
    def _():
        fin[group, 0:2] = res[win, 0:2]
        others = fin.at[0:groups - 1, 0:2]
        pltpu.make_async_copy(others, others, f_recv.at[0]).wait()

    @pl.when(core == 1)
    def _():
        fin[group, 0:1] = res[win, 2:3]
        others = fin.at[0:groups - 1, 0:1]
        pltpu.make_async_copy(others, others, f_recv.at[0]).wait()

    everyone = fin.at[:, 2:3]
    pltpu.make_async_copy(everyone, everyone, f_recv.at[1]).wait()

    first = fin[:, 0].astype(jnp.float32).reshape(CH, 128)
    third = fin[:, 1].astype(jnp.float32).reshape(CH, 128)
    last = fin[:, 2].astype(jnp.float32).reshape(CH, 128)
    wide_lanes = lax.broadcasted_iota(jnp.int32, (CH, 128), 1)
    second = jnp.where((wide_lanes < 64) & (core == 0), third, last)
    first, second = first.T, second.T
    choices = (first[:64], first[64:], second[:64], second[64:])
    for slot in range(4):
        offset = off_ref[0, slot]
        picked = choices[3]
        for index in range(3):
            picked = jnp.where(offset == index + 1, choices[index], picked)
        weight = mask_ref[slot:slot + 1, :].astype(jnp.float32)
        picked = jnp.where(slot < cnt_ref[0, 0], picked * weight, 0.0)
        out_ref[pl.ds(slot, 64, stride=4), :] = picked

    def finish(step, carry):
        there, side = step // 2, step % 2

        @pl.when(step != group)
        def _():
            for half in range(HALVES):
                exchange(half, there, side).wait_send()
        return carry

    lax.fori_loop(0, groups, finish, 0)

    def finish_rest(step, carry):
        forward(step, True).wait_send()
        forward(step, False).wait_send()
        for kind in range(4):
            if kind < 2:
                @pl.when((step != win) | (core != kind))
                def _():
                    deliver(step, kind).wait_send()
            else:
                deliver(step, kind).wait_send()
        return carry

    lax.fori_loop(0, wins, finish_rest, 0)


def local(chips, wins, windows, pair_offset, pair_count, pair_mask):
    groups = 2 * wins
    fwd_table = jnp.asarray(forward_table())
    factor = 1.0 / (LENGTH * math.sqrt(FB * windows.shape[0] * wins))
    hbm = pl.BlockSpec(memory_space=pltpu.HBM)
    smem = pl.BlockSpec(memory_space=pltpu.SMEM)
    vmem = pl.BlockSpec(memory_space=pltpu.VMEM)
    out = pl.pallas_call(
        functools.partial(kernel, chips, wins, factor),
        out_shape=jax.ShapeDtypeStruct((LAGS // wins * 4, CH), jnp.float32),
        in_specs=[hbm, hbm, vmem, smem, smem, vmem],
        out_specs=vmem,
        scratch_shapes=[
            pltpu.VMEM((LENGTH, CH), jnp.bfloat16),
            pltpu.VMEM(fwd_table.shape, jnp.bfloat16),
            pltpu.VMEM((HALVES, groups, ROWS, 2 * FB // HALVES), jnp.bfloat16),
            pltpu.VMEM((3, wins, 2, HALVES, ROWS, 2 * FB // HALVES), jnp.bfloat16),
            pltpu.VMEM((len(PAIRS) * ROWS, 2 * FB), jnp.float32),
            pltpu.VMEM((wins, len(TILES), ROWS, 128), SEND),
            pltpu.VMEM((groups, 3, ROWS, 128), SEND),
            pltpu.SemaphoreType.DMA((1 + QUARTERS,)),
            pltpu.SemaphoreType.DMA((HALVES, wins, 2)),
            pltpu.SemaphoreType.DMA((HALVES, wins, 2)),
            pltpu.SemaphoreType.DMA((2, wins)),
            pltpu.SemaphoreType.DMA((2, wins)),
            pltpu.SemaphoreType.DMA((4, wins)),
            pltpu.SemaphoreType.DMA((2,)),
        ],
        compiler_params=pltpu.CompilerParams(
            collective_id=0, has_side_effects=True
        ),
        name="correlate",
    )(windows, fwd_table, jnp.asarray(lag_turns()), pair_offset, pair_count.reshape(1, 1), pair_mask)
    return out.reshape(LAGS // wins, 4, CH)


def solution(mesh):
    chips, wins = mesh.shape["pair"] // 2, mesh.shape["win"]
    placed = (P("win", None, "pair"), P("pair", None), P("pair"), P("pair", None))
    return jax.shard_map(
        functools.partial(local, chips, wins),
        mesh=mesh,
        in_specs=placed,
        out_specs=P("win", "pair", None),
        check_vma=False,
    )
```

```python
import functools
import math

import jax
import jax.numpy as jnp
import numpy as np
from jax import lax
from jax.experimental import pallas as pl
from jax.experimental.pallas import tpu as pltpu
from jax.sharding import PartitionSpec as P

FB = 512
F0 = 64
LAGS = 512
LENGTH = 2048
CH = 128
SPLIT = 4
FOLD = LENGTH // SPLIT
QUARTERS = 4
HALVES = 2
ROWS = 8
SEND = jnp.bfloat16
MESH = pl.DeviceIdType.MESH
ROW = 8
OWN_PAIRS = ((2, 3), (2, 4), (2, 5), (3, 4), (3, 5))
BEFORE_PAIRS = ((0, 4), (1, 4), (1, 5))
BEYOND_PAIRS = ((2, 6), (3, 6), (3, 7))
COUNT = 12
TILES = ((0, 1), (2, 2), (3, 4), (5, 5), (6, 7), (8, 8), (9, 10))


def quarter_bins(quarter):
    steps = 8 * np.arange(FB // 8)
    return np.concatenate([steps + 2 * quarter, steps + 2 * quarter + 1])


def two_parts(table):
    high = table.astype(jnp.bfloat16)
    rest = (table - high.astype(np.float64)).astype(jnp.bfloat16)
    return high, rest


def forward_table():
    nfft = 2 * LENGTH
    parts = []
    for quarter in range(QUARTERS):
        phase = 2 * np.pi * ((F0 + quarter_bins(quarter))[:, None] * np.arange(FOLD)[None, :] % nfft) / nfft
        table = np.concatenate([np.cos(phase), -np.sin(phase)], axis=0)
        parts.append(np.concatenate(two_parts(table), axis=1))
    return np.stack(parts)


def lag_turns():
    bins = np.concatenate([quarter_bins(quarter) for quarter in range(QUARTERS)])
    phase = 2 * np.pi * ((F0 + bins) * (LAGS // 2) % (2 * LENGTH)) / (2 * LENGTH)
    return np.stack([np.cos(phase), np.sin(phase)]).astype(np.float32)


def weighted(terms):
    total = None
    for weight, value in terms:
        if abs(weight) < 1e-9:
            continue
        if abs(abs(weight) - 1.0) > 1e-9:
            value = value * np.float32(abs(weight))
        if total is None:
            total = value if weight > 0 else -value
        else:
            total = total + value if weight > 0 else total - value
    return total


def kernel(
    chips, wins, factor, x_hbm, fwd_hbm, turn_ref, off_ref, cnt_ref, mask_ref, out_ref,
    xbuf, fwd, spec, gath, acc, res, fin,
    load_sem, a_send, a_recv, z_send, z_recv, f_send, f_recv, ready,
):
    pair, win = lax.axis_index("pair"), lax.axis_index("win")
    chip, core = pair // 2, pair % 2
    place = chip % ROW
    low = place == 0
    high = (place == ROW - 1) | (chip == chips - 1)
    has_before, has_after = chip > 0, chip < chips - 1
    group = win * 2 + core
    groups = 2 * wins
    tiles = len(TILES)

    def device(chip_shift, side, there):
        return (2 * (chip + chip_shift) + side, there)

    x_copy = pltpu.make_async_copy(x_hbm.at[0], xbuf, load_sem.at[0])
    x_copy.start()
    fwd_copies = []
    for quarter in range(QUARTERS):
        copy = pltpu.make_async_copy(fwd_hbm.at[quarter], fwd.at[quarter], load_sem.at[1 + quarter])
        copy.start()
        fwd_copies.append(copy)

    barrier = pltpu.get_barrier_semaphore()

    def greet(step, carry):
        there, side = (win + step // 2) % wins, (core + step % 2) % 2

        @pl.when(step > 0)
        def _():
            pl.semaphore_signal(barrier, inc=1, device_id=device(0, side, there), device_id_type=MESH)

        @pl.when(jnp.logical_not(high))
        def _():
            pl.semaphore_signal(barrier, inc=1, device_id=device(1, side, there), device_id_type=MESH)
        return carry

    lax.fori_loop(0, groups, greet, 0)

    @pl.when(low & has_before)
    def _():
        pl.semaphore_signal(barrier, inc=1, device_id=device(-1, core, win), device_id_type=MESH)

    acc[...] = jnp.zeros_like(acc)

    @pl.when(jnp.logical_not(has_after))
    def _():
        gath[2:4] = jnp.zeros_like(gath[2:4])

    def near(step):
        turn = (step % 2) * ((step + 1) // 2) + (1 - step % 2) * (wins - step // 2)
        return (win + turn) % wins

    def exchange(half, there, side):
        return pltpu.make_async_remote_copy(
            src_ref=spec.at[half, there * 2 + side],
            dst_ref=gath.at[1, win, core, half],
            send_sem=a_send,
            recv_sem=a_recv.at[win],
            device_id=device(0, side, there),
            device_id_type=MESH,
        )

    def settle(ref, sem):
        pltpu.make_async_copy(ref, ref, sem).wait()

    x_copy.wait()
    for half in range(HALVES):
        for part in range(QUARTERS // HALVES):
            quarter = half * (QUARTERS // HALVES) + part
            fwd_copies[quarter].wait()
            wide = jnp.concatenate([xbuf[h * FOLD:(h + 1) * FOLD, :] for h in range(SPLIT)], axis=1)
            whole = jnp.dot(fwd[quarter, :, :FOLD], wide, preferred_element_type=jnp.float32)
            whole += jnp.dot(fwd[quarter, :, FOLD:], wide, preferred_element_type=jnp.float32)
            reals, imags = [], []
            for odd in range(2):
                residue = 2 * quarter + odd
                real_terms, imag_terms = [], []
                for h in range(SPLIT):
                    turn = 2 * math.pi * ((residue * h) % 8) / 8
                    real = whole[odd * 64:odd * 64 + 64, h * CH:(h + 1) * CH]
                    imag = whole[128 + odd * 64:128 + odd * 64 + 64, h * CH:(h + 1) * CH]
                    real_terms += [(math.cos(turn), real), (math.sin(turn), imag)]
                    imag_terms += [(math.cos(turn), imag), (-math.sin(turn), real)]
                reals.append(weighted(real_terms))
                imags.append(weighted(imag_terms))
            for kind, value in enumerate((reals, imags)):
                turned = jnp.concatenate(value, axis=0).T.reshape(groups, ROWS, 128)
                lane = part * 256 + kind * 128
                spec[half, :, :, lane:lane + 128] = turned.astype(jnp.bfloat16)
        if half == 0:
            later = jnp.where(high & has_after, 1, 0)
            pl.semaphore_wait(barrier, groups - 1 + jnp.where(low, 0, groups) + later)

            @pl.when(jnp.logical_not(low))
            def _():
                pl.semaphore_signal(ready.at[0], inc=1, device_id=device(-1, core, win), device_id_type=MESH)

            @pl.when(high & has_after)
            def _():
                pl.semaphore_signal(ready.at[1], inc=1, device_id=device(1, core, win), device_id_type=MESH)

        def send(step, carry, half=half):
            exchange(half, near(step // 2), (core + step % 2) % 2).start()
            return carry

        lax.fori_loop(1, groups, send, 0)
        gath[1, win, core, half] = spec[half, group]

    def forward(there, kind):
        return pltpu.make_async_remote_copy(
            src_ref=gath.at[(1, 1, 2)[kind], there],
            dst_ref=gath.at[(0, 2, 3)[kind], there],
            send_sem=z_send.at[kind],
            recv_sem=z_recv.at[kind, there],
            device_id=device((1, -1, -1)[kind], core, win),
            device_id_type=MESH,
        )

    def multiply(there, pairs, base):
        used = sorted({block for both in pairs for block in both})
        for quarter in range(QUARTERS):
            half, lane = quarter // (QUARTERS // HALVES), quarter % (QUARTERS // HALVES) * 256
            blocks = {}
            for block in used:
                both = gath[block // 2, there, block % 2, half, :, lane:lane + 256].astype(jnp.float32)
                blocks[block] = (both[:, :128], both[:, 128:])
            for index, (own, other) in enumerate(pairs):
                (own_real, own_imag), (other_real, other_imag) = blocks[own], blocks[other]
                rows = slice((base + index) * ROWS, (base + index + 1) * ROWS)
                left = slice(quarter * 256, quarter * 256 + 128)
                right = slice(quarter * 256 + 128, quarter * 256 + 256)
                acc[rows, left] += own_real * other_real + own_imag * other_imag
                acc[rows, right] += own_imag * other_real - own_real * other_imag

    lag = 3

    def travel(step, carry):
        @pl.when(step < wins)
        def _():
            there = near(step)

            @pl.when(step == 0)
            def _():
                settle(gath.at[1, win, 1 - core], a_recv.at[win])

            @pl.when(step > 0)
            def _():
                settle(gath.at[1, there], a_recv.at[there])

            @pl.when(jnp.logical_not(high))
            def _():
                @pl.when(step == 0)
                def _():
                    pl.semaphore_wait(ready.at[0], 1)

                forward(there, 0).start()

            @pl.when(has_before)
            def _():
                @pl.when(low & (step == 0))
                def _():
                    pl.semaphore_wait(ready.at[1], 1)

                forward(there, 1).start()

        @pl.when(step >= lag)
        def _():
            there = near(step - lag)

            @pl.when(has_after)
            def _():
                forward(there, 1).wait_recv()

            @pl.when(low & has_before)
            def _():
                forward(there, 2).start()

            multiply(there, OWN_PAIRS, 0)

            @pl.when(jnp.logical_not(low))
            def _():
                forward(there, 0).wait_recv()
                multiply(there, BEFORE_PAIRS, len(OWN_PAIRS))

            @pl.when(high & has_after)
            def _():
                forward(there, 2).wait_recv()
                multiply(there, BEYOND_PAIRS, len(OWN_PAIRS) + len(BEFORE_PAIRS))
        return carry

    lax.fori_loop(0, wins + lag, travel, 0)

    count = COUNT * ROWS
    stacks = jnp.zeros((count, LAGS), jnp.float32)
    for quarter in range(QUARTERS):
        bins = slice(quarter * 128, quarter * 128 + 128)
        cosine, sine = turn_ref[0:1, bins] * factor, turn_ref[1:2, bins] * factor
        real = acc[:, quarter * 256:quarter * 256 + 128]
        imag = acc[:, quarter * 256 + 128:quarter * 256 + 256]
        cross = jnp.concatenate([real * cosine + imag * sine, imag * cosine - real * sine], axis=1)
        high_part = cross.astype(jnp.bfloat16)
        rest = (cross - high_part.astype(jnp.float32)).astype(jnp.bfloat16)
        both = jnp.concatenate([high_part, rest], axis=0)
        upper = jnp.dot(both, fwd[quarter, :, :FOLD], preferred_element_type=jnp.float32)
        stacks += upper[:count] + upper[count:]
        stacks += jnp.dot(high_part, fwd[quarter, :, FOLD:], preferred_element_type=jnp.float32)
    lanes = lax.broadcasted_iota(jnp.int32, (ROWS, 128), 1)
    for column in range(LAGS // 128):
        for tile, (left, right) in enumerate(TILES):
            a = stacks[left * ROWS:(left + 1) * ROWS, column * 128:(column + 1) * 128]
            b = stacks[right * ROWS:(right + 1) * ROWS, column * 128:(column + 1) * 128]
            even = jnp.where(lanes < 64, a, pltpu.roll(b, 64, 1))
            odd = jnp.where(lanes < 64, pltpu.roll(a, 64, 1), b)
            res[2 * column * tiles + tile] = even.astype(SEND)
            res[(2 * column + 1) * tiles + tile] = odd.astype(SEND)

    def deliver(there, kind):
        first, size, slot = ((0, 2, 0), (2, 1, 0), (3, 1, 2), (4, 1, 2), (5, 1, 2), (6, 1, 2))[kind]
        return pltpu.make_async_remote_copy(
            src_ref=res.at[pl.ds(there * tiles + first, size)],
            dst_ref=fin.at[group, slot:slot + size],
            send_sem=f_send.at[kind // 2],
            recv_sem=f_recv.at[0 if kind < 2 else 1],
            device_id=device(-1 if kind // 2 == 1 else 0, kind % 2, there),
            device_id_type=MESH,
        )

    def hand_out(step, carry):
        there = near(step)

        @pl.when(jnp.logical_not(low))
        def _():
            deliver(there, 2).start()
            deliver(there, 3).start()

        for side in range(2):
            @pl.when((step > 0) | (core != side))
            def _():
                deliver(there, side).start()

                @pl.when(high)
                def _():
                    deliver(there, 4 + side).start()
        return carry

    lax.fori_loop(0, wins, hand_out, 0)
    mine = win * tiles

    @pl.when(core == 0)
    def _():
        fin[group, 0:2] = res[pl.ds(mine, 2)]

    @pl.when(core == 1)
    def _():
        fin[group, 0:1] = res[pl.ds(mine + 2, 1)]

    @pl.when(high)
    def _():
        fin[group, 2:3] = res[pl.ds(mine + 5 + core, 1)]

    settle(spec.at[:, 0:groups - 1], a_send)

    @pl.when(jnp.logical_not(high))
    def _():
        settle(gath.at[1], z_send.at[0])

    @pl.when(has_before)
    def _():
        settle(gath.at[1], z_send.at[1])

    @pl.when(low & has_before)
    def _():
        settle(gath.at[1], z_send.at[2])

    @pl.when(core == 0)
    def _():
        settle(fin.at[0:groups - 1, 0:2], f_recv.at[0])

    @pl.when(core == 1)
    def _():
        settle(fin.at[0:groups - 1, 0:1], f_recv.at[0])

    @pl.when(high)
    def _():
        settle(fin.at[0:groups - 1, 2:3], f_recv.at[1])

    @pl.when(jnp.logical_not(high))
    def _():
        settle(fin.at[:, 2:3], f_recv.at[1])

    first = fin[:, 0].astype(jnp.float32).reshape(CH, 128)
    third = fin[:, 1].astype(jnp.float32).reshape(CH, 128)
    last = fin[:, 2].astype(jnp.float32).reshape(CH, 128)
    wide_lanes = lax.broadcasted_iota(jnp.int32, (CH, 128), 1)
    second = jnp.where((wide_lanes < 64) & (core == 0), third, last)
    first, second = first.T, second.T
    choices = (first[:64], first[64:], second[:64], second[64:])
    for slot in range(4):
        offset = off_ref[0, slot]
        picked = choices[3]
        for index in range(3):
            picked = jnp.where(offset == index + 1, choices[index], picked)
        weight = mask_ref[slot:slot + 1, :].astype(jnp.float32)
        picked = jnp.where(slot < cnt_ref[0, 0], picked * weight, 0.0)
        out_ref[pl.ds(slot, 64, stride=4), :] = picked

    @pl.when(core == 0)
    def _():
        settle(res.at[0:3 * wins - 2], f_send.at[0])

    @pl.when(core == 1)
    def _():
        settle(res.at[0:3 * wins - 1], f_send.at[0])

    @pl.when(jnp.logical_not(low))
    def _():
        settle(res.at[0:groups], f_send.at[1])

    @pl.when(high)
    def _():
        settle(res.at[0:groups - 1], f_send.at[2])


def local(chips, wins, windows, pair_offset, pair_count, pair_mask):
    groups = 2 * wins
    fwd_table = jnp.asarray(forward_table())
    factor = 1.0 / (LENGTH * math.sqrt(FB * windows.shape[0] * wins))
    hbm = pl.BlockSpec(memory_space=pltpu.HBM)
    smem = pl.BlockSpec(memory_space=pltpu.SMEM)
    vmem = pl.BlockSpec(memory_space=pltpu.VMEM)
    out = pl.pallas_call(
        functools.partial(kernel, chips, wins, factor),
        out_shape=jax.ShapeDtypeStruct((LAGS // wins * 4, CH), jnp.float32),
        in_specs=[hbm, hbm, vmem, smem, smem, vmem],
        out_specs=vmem,
        scratch_shapes=[
            pltpu.VMEM((LENGTH, CH), jnp.bfloat16),
            pltpu.VMEM(fwd_table.shape, jnp.bfloat16),
            pltpu.VMEM((HALVES, groups, ROWS, 2 * FB // HALVES), jnp.bfloat16),
            pltpu.VMEM((4, wins, 2, HALVES, ROWS, 2 * FB // HALVES), jnp.bfloat16),
            pltpu.VMEM((COUNT * ROWS, 2 * FB), jnp.float32),
            pltpu.VMEM((wins * len(TILES), ROWS, 128), SEND),
            pltpu.VMEM((groups, 3, ROWS, 128), SEND),
            pltpu.SemaphoreType.DMA((1 + QUARTERS,)),
            pltpu.SemaphoreType.DMA,
            pltpu.SemaphoreType.DMA((wins,)),
            pltpu.SemaphoreType.DMA((3,)),
            pltpu.SemaphoreType.DMA((3, wins)),
            pltpu.SemaphoreType.DMA((3,)),
            pltpu.SemaphoreType.DMA((2,)),
            pltpu.SemaphoreType.REGULAR((2,)),
        ],
        compiler_params=pltpu.CompilerParams(
            collective_id=0, has_side_effects=True
        ),
        name="correlate",
    )(windows, fwd_table, jnp.asarray(lag_turns()), pair_offset, pair_count.reshape(1, 1), pair_mask)
    return out.reshape(LAGS // wins, 4, CH)


def solution(mesh):
    chips, wins = mesh.shape["pair"] // 2, mesh.shape["win"]
    placed = (P("win", None, "pair"), P("pair", None), P("pair"), P("pair", None))
    return jax.shard_map(
        functools.partial(local, chips, wins),
        mesh=mesh,
        in_specs=placed,
        out_specs=P("win", "pair", None),
        check_vma=False,
    )
```

```python
import functools
import math

import jax
import jax.numpy as jnp
import numpy as np
from jax import lax
from jax.experimental import pallas as pl
from jax.experimental.pallas import tpu as pltpu
from jax.sharding import PartitionSpec as P

FB = 512
F0 = 64
LAGS = 512
LENGTH = 2048
CH = 128
SPLIT = 4
FOLD = LENGTH // SPLIT
QUARTERS = 4
HALVES = 1
ROWS = 8
SEND = jnp.bfloat16
MESH = pl.DeviceIdType.MESH
ROW = 8
OWN_PAIRS = ((2, 3), (2, 4), (2, 5), (3, 4), (3, 5))
BEFORE_PAIRS = ((0, 4), (1, 4), (1, 5))
BEYOND_PAIRS = ((2, 6), (3, 6), (3, 7))
COUNT = 12
TILES = ((0, 1), (2, 2), (3, 4), (5, 5), (6, 7), (8, 8), (9, 10))


def quarter_bins(quarter):
    steps = 8 * np.arange(FB // 8)
    return np.concatenate([steps + 2 * quarter, steps + 2 * quarter + 1])


def two_parts(table):
    high = table.astype(jnp.bfloat16)
    rest = (table - high.astype(np.float64)).astype(jnp.bfloat16)
    return high, rest


def forward_table():
    nfft = 2 * LENGTH
    parts = []
    for quarter in range(QUARTERS):
        phase = 2 * np.pi * ((F0 + quarter_bins(quarter))[:, None] * np.arange(FOLD)[None, :] % nfft) / nfft
        table = np.concatenate([np.cos(phase), -np.sin(phase)], axis=0)
        parts.append(np.concatenate(two_parts(table), axis=1))
    return np.stack(parts)


def lag_turns():
    bins = np.concatenate([quarter_bins(quarter) for quarter in range(QUARTERS)])
    phase = 2 * np.pi * ((F0 + bins) * (LAGS // 2) % (2 * LENGTH)) / (2 * LENGTH)
    return np.stack([np.cos(phase), np.sin(phase)]).astype(np.float32)


def weighted(terms):
    total = None
    for weight, value in terms:
        if abs(weight) < 1e-9:
            continue
        if abs(abs(weight) - 1.0) > 1e-9:
            value = value * np.float32(abs(weight))
        if total is None:
            total = value if weight > 0 else -value
        else:
            total = total + value if weight > 0 else total - value
    return total


def kernel(
    chips, wins, factor, x_hbm, fwd_hbm, turn_hbm, off_hbm, mask_hbm, cnt_ref, out_ref,
    xbuf, fwd, turn_ref, off_ref, mask_ref, spec, gath, acc, res, fin,
    load_sem, a_send, a_recv, z_send, z_recv, f_send, f_recv, ready,
):
    pair, win = lax.axis_index("pair"), lax.axis_index("win")
    chip, core = pair // 2, pair % 2
    place = chip % ROW
    low = place == 0
    high = (place == ROW - 1) | (chip == chips - 1)
    has_before, has_after = chip > 0, chip < chips - 1
    group = win * 2 + core
    groups = 2 * wins
    tiles = len(TILES)

    def device(chip_shift, side, there):
        return (2 * (chip + chip_shift) + side, there)

    x_copy = pltpu.make_async_copy(x_hbm.at[0], xbuf, load_sem.at[0])
    x_copy.start()
    fwd_copies = []
    for quarter in range(QUARTERS):
        copy = pltpu.make_async_copy(fwd_hbm.at[quarter], fwd.at[quarter], load_sem.at[1 + quarter])
        copy.start()
        fwd_copies.append(copy)
    small_copies = []
    for source, target in ((turn_hbm, turn_ref), (off_hbm, off_ref), (mask_hbm, mask_ref)):
        copy = pltpu.make_async_copy(source, target, load_sem.at[1 + QUARTERS + len(small_copies)])
        copy.start()
        small_copies.append(copy)

    barrier = pltpu.get_barrier_semaphore()

    def greet(step, carry):
        there, side = (win + step // 2) % wins, (core + step % 2) % 2

        @pl.when(step > 0)
        def _():
            pl.semaphore_signal(barrier, inc=1, device_id=device(0, side, there), device_id_type=MESH)

        @pl.when(jnp.logical_not(high))
        def _():
            pl.semaphore_signal(barrier, inc=1, device_id=device(1, side, there), device_id_type=MESH)
        return carry

    lax.fori_loop(0, groups, greet, 0)

    @pl.when(low & has_before)
    def _():
        pl.semaphore_signal(barrier, inc=1, device_id=device(-1, core, win), device_id_type=MESH)

    acc[...] = jnp.zeros_like(acc)

    @pl.when(jnp.logical_not(has_after))
    def _():
        gath[2:4] = jnp.zeros_like(gath[2:4])

    def near(step):
        turn = (step % 2) * ((step + 1) // 2) + (1 - step % 2) * (wins - step // 2)
        return (win + turn) % wins

    def exchange(half, there, side):
        return pltpu.make_async_remote_copy(
            src_ref=spec.at[half, there * 2 + side],
            dst_ref=gath.at[1, win, core, half],
            send_sem=a_send,
            recv_sem=a_recv.at[win],
            device_id=device(0, side, there),
            device_id_type=MESH,
        )

    def settle(ref, sem):
        pltpu.make_async_copy(ref, ref, sem).wait()

    x_copy.wait()
    for half in range(HALVES):
        for part in range(QUARTERS // HALVES):
            quarter = half * (QUARTERS // HALVES) + part
            fwd_copies[quarter].wait()
            wide = jnp.concatenate([xbuf[h * FOLD:(h + 1) * FOLD, :] for h in range(SPLIT)], axis=1)
            whole = jnp.dot(fwd[quarter, :, :FOLD], wide, preferred_element_type=jnp.float32)
            whole += jnp.dot(fwd[quarter, :, FOLD:], wide, preferred_element_type=jnp.float32)
            reals, imags = [], []
            for odd in range(2):
                residue = 2 * quarter + odd
                real_terms, imag_terms = [], []
                for h in range(SPLIT):
                    turn = 2 * math.pi * ((residue * h) % 8) / 8
                    real = whole[odd * 64:odd * 64 + 64, h * CH:(h + 1) * CH]
                    imag = whole[128 + odd * 64:128 + odd * 64 + 64, h * CH:(h + 1) * CH]
                    real_terms += [(math.cos(turn), real), (math.sin(turn), imag)]
                    imag_terms += [(math.cos(turn), imag), (-math.sin(turn), real)]
                reals.append(weighted(real_terms))
                imags.append(weighted(imag_terms))
            for kind, value in enumerate((reals, imags)):
                turned = jnp.concatenate(value, axis=0).T.reshape(groups, ROWS, 128)
                lane = part * 256 + kind * 128
                spec[half, :, :, lane:lane + 128] = turned.astype(jnp.bfloat16)
        if half == 0:
            later = jnp.where(high & has_after, 1, 0)
            pl.semaphore_wait(barrier, groups - 1 + jnp.where(low, 0, groups) + later)

            @pl.when(jnp.logical_not(low))
            def _():
                pl.semaphore_signal(ready.at[0], inc=1, device_id=device(-1, core, win), device_id_type=MESH)

            @pl.when(high & has_after)
            def _():
                pl.semaphore_signal(ready.at[1], inc=1, device_id=device(1, core, win), device_id_type=MESH)

        def send(step, carry, half=half):
            exchange(half, near(step // 2), (core + step % 2) % 2).start()
            return carry

        lax.fori_loop(1, groups, send, 0)
        gath[1, win, core, half] = spec[half, group]

    def forward(there, kind):
        return pltpu.make_async_remote_copy(
            src_ref=gath.at[(1, 1, 2)[kind], there],
            dst_ref=gath.at[(0, 2, 3)[kind], there],
            send_sem=z_send.at[kind],
            recv_sem=z_recv.at[kind, there],
            device_id=device((1, -1, -1)[kind], core, win),
            device_id_type=MESH,
        )

    def multiply(there, pairs, base):
        used = sorted({block for both in pairs for block in both})
        for quarter in range(QUARTERS):
            half, lane = quarter // (QUARTERS // HALVES), quarter % (QUARTERS // HALVES) * 256
            blocks = {}
            for block in used:
                both = gath[block // 2, there, block % 2, half, :, lane:lane + 256].astype(jnp.float32)
                blocks[block] = (both[:, :128], both[:, 128:])
            for index, (own, other) in enumerate(pairs):
                (own_real, own_imag), (other_real, other_imag) = blocks[own], blocks[other]
                rows = slice((base + index) * ROWS, (base + index + 1) * ROWS)
                left = slice(quarter * 256, quarter * 256 + 128)
                right = slice(quarter * 256 + 128, quarter * 256 + 256)
                acc[rows, left] += own_real * other_real + own_imag * other_imag
                acc[rows, right] += own_imag * other_real - own_real * other_imag

    lag = 6

    def travel(step, carry):
        @pl.when(step < wins)
        def _():
            there = near(step)

            @pl.when(step == 0)
            def _():
                settle(gath.at[1, win, 1 - core], a_recv.at[win])

            @pl.when(step > 0)
            def _():
                settle(gath.at[1, there], a_recv.at[there])

            @pl.when(jnp.logical_not(high))
            def _():
                @pl.when(step == 0)
                def _():
                    pl.semaphore_wait(ready.at[0], 1)

                forward(there, 0).start()

            @pl.when(has_before)
            def _():
                @pl.when(low & (step == 0))
                def _():
                    pl.semaphore_wait(ready.at[1], 1)

                forward(there, 1).start()

        @pl.when(step >= lag)
        def _():
            there = near(step - lag)

            @pl.when(has_after)
            def _():
                forward(there, 1).wait_recv()

            @pl.when(low & has_before)
            def _():
                forward(there, 2).start()

            multiply(there, OWN_PAIRS, 0)

            @pl.when(jnp.logical_not(low))
            def _():
                forward(there, 0).wait_recv()
                multiply(there, BEFORE_PAIRS, len(OWN_PAIRS))

            @pl.when(high & has_after)
            def _():
                forward(there, 2).wait_recv()
                multiply(there, BEYOND_PAIRS, len(OWN_PAIRS) + len(BEFORE_PAIRS))
        return carry

    lax.fori_loop(0, wins + lag, travel, 0)

    for copy in small_copies:
        copy.wait()
    count = COUNT * ROWS
    stacks = jnp.zeros((count, LAGS), jnp.float32)
    for quarter in range(QUARTERS):
        bins = slice(quarter * 128, quarter * 128 + 128)
        cosine, sine = turn_ref[0:1, bins] * factor, turn_ref[1:2, bins] * factor
        real = acc[:, quarter * 256:quarter * 256 + 128]
        imag = acc[:, quarter * 256 + 128:quarter * 256 + 256]
        cross = jnp.concatenate([real * cosine + imag * sine, imag * cosine - real * sine], axis=1)
        high_part = cross.astype(jnp.bfloat16)
        rest = (cross - high_part.astype(jnp.float32)).astype(jnp.bfloat16)
        both = jnp.concatenate([high_part, rest], axis=0)
        upper = jnp.dot(both, fwd[quarter, :, :FOLD], preferred_element_type=jnp.float32)
        stacks += upper[:count] + upper[count:]
        stacks += jnp.dot(high_part, fwd[quarter, :, FOLD:], preferred_element_type=jnp.float32)
    lanes = lax.broadcasted_iota(jnp.int32, (ROWS, 128), 1)
    for column in range(LAGS // 128):
        for tile, (left, right) in enumerate(TILES):
            a = stacks[left * ROWS:(left + 1) * ROWS, column * 128:(column + 1) * 128]
            b = stacks[right * ROWS:(right + 1) * ROWS, column * 128:(column + 1) * 128]
            even = jnp.where(lanes < 64, a, pltpu.roll(b, 64, 1))
            odd = jnp.where(lanes < 64, pltpu.roll(a, 64, 1), b)
            res[2 * column * tiles + tile] = even.astype(SEND)
            res[(2 * column + 1) * tiles + tile] = odd.astype(SEND)

    def deliver(there, kind):
        first, size, slot = ((0, 2, 0), (2, 1, 0), (3, 1, 2), (4, 1, 2), (5, 1, 2), (6, 1, 2))[kind]
        return pltpu.make_async_remote_copy(
            src_ref=res.at[pl.ds(there * tiles + first, size)],
            dst_ref=fin.at[group, slot:slot + size],
            send_sem=f_send.at[kind // 2],
            recv_sem=f_recv.at[0 if kind < 2 else 1],
            device_id=device(-1 if kind // 2 == 1 else 0, kind % 2, there),
            device_id_type=MESH,
        )

    def hand_out(step, carry):
        there = near(wins - 1 - step)

        @pl.when(jnp.logical_not(low))
        def _():
            deliver(there, 2).start()
            deliver(there, 3).start()

        for side in range(2):
            @pl.when((step < wins - 1) | (core != side))
            def _():
                deliver(there, side).start()

                @pl.when(high)
                def _():
                    deliver(there, 4 + side).start()
        return carry

    lax.fori_loop(0, wins, hand_out, 0)
    mine = win * tiles

    @pl.when(core == 0)
    def _():
        fin[group, 0:2] = res[pl.ds(mine, 2)]

    @pl.when(core == 1)
    def _():
        fin[group, 0:1] = res[pl.ds(mine + 2, 1)]

    @pl.when(high)
    def _():
        fin[group, 2:3] = res[pl.ds(mine + 5 + core, 1)]

    settle(spec.at[:, 0:groups - 1], a_send)

    @pl.when(jnp.logical_not(high))
    def _():
        settle(gath.at[1], z_send.at[0])

    @pl.when(has_before)
    def _():
        settle(gath.at[1], z_send.at[1])

    @pl.when(low & has_before)
    def _():
        settle(gath.at[1], z_send.at[2])

    @pl.when(core == 0)
    def _():
        settle(fin.at[0:groups - 1, 0:2], f_recv.at[0])

    @pl.when(core == 1)
    def _():
        settle(fin.at[0:groups - 1, 0:1], f_recv.at[0])

    @pl.when(high)
    def _():
        settle(fin.at[0:groups - 1, 2:3], f_recv.at[1])

    @pl.when(jnp.logical_not(high))
    def _():
        settle(fin.at[:, 2:3], f_recv.at[1])

    first = fin[:, 0].astype(jnp.float32).reshape(CH, 128)
    third = fin[:, 1].astype(jnp.float32).reshape(CH, 128)
    last = fin[:, 2].astype(jnp.float32).reshape(CH, 128)
    wide_lanes = lax.broadcasted_iota(jnp.int32, (CH, 128), 1)
    second = jnp.where((wide_lanes < 64) & (core == 0), third, last)
    first, second = first.T, second.T
    choices = (first[:64], first[64:], second[:64], second[64:])
    for slot in range(4):
        offset = off_ref[0, slot]
        picked = choices[3]
        for index in range(3):
            picked = jnp.where(offset == index + 1, choices[index], picked)
        weight = mask_ref[slot:slot + 1, :].astype(jnp.float32)
        picked = jnp.where(slot < cnt_ref[0, 0], picked * weight, 0.0)
        out_ref[pl.ds(slot, 64, stride=4), :] = picked

    @pl.when(core == 0)
    def _():
        settle(res.at[0:3 * wins - 2], f_send.at[0])

    @pl.when(core == 1)
    def _():
        settle(res.at[0:3 * wins - 1], f_send.at[0])

    @pl.when(jnp.logical_not(low))
    def _():
        settle(res.at[0:groups], f_send.at[1])

    @pl.when(high)
    def _():
        settle(res.at[0:groups - 1], f_send.at[2])


def local(chips, wins, windows, pair_offset, pair_count, pair_mask):
    groups = 2 * wins
    fwd_table = jnp.asarray(forward_table())
    factor = 1.0 / (LENGTH * math.sqrt(FB * windows.shape[0] * wins))
    hbm = pl.BlockSpec(memory_space=pltpu.HBM)
    operands = (windows, fwd_table, jnp.asarray(lag_turns()), pair_offset, pair_mask)
    vmem = pl.BlockSpec(memory_space=pltpu.VMEM)
    out = pl.pallas_call(
        functools.partial(kernel, chips, wins, factor),
        out_shape=jax.ShapeDtypeStruct((LAGS // wins * 4, CH), jnp.float32),
        in_specs=[hbm] * len(operands) + [pl.BlockSpec(memory_space=pltpu.SMEM)],
        out_specs=vmem,
        scratch_shapes=[
            pltpu.VMEM((LENGTH, CH), jnp.bfloat16),
            pltpu.VMEM(fwd_table.shape, jnp.bfloat16),
            pltpu.VMEM((2, FB), jnp.float32),
            pltpu.SMEM(pair_offset.shape, jnp.int32),
            pltpu.VMEM(pair_mask.shape, jnp.int32),
            pltpu.VMEM((HALVES, groups, ROWS, 2 * FB // HALVES), jnp.bfloat16),
            pltpu.VMEM((4, wins, 2, HALVES, ROWS, 2 * FB // HALVES), jnp.bfloat16),
            pltpu.VMEM((COUNT * ROWS, 2 * FB), jnp.float32),
            pltpu.VMEM((wins * len(TILES), ROWS, 128), SEND),
            pltpu.VMEM((groups, 3, ROWS, 128), SEND),
            pltpu.SemaphoreType.DMA((4 + QUARTERS,)),
            pltpu.SemaphoreType.DMA,
            pltpu.SemaphoreType.DMA((wins,)),
            pltpu.SemaphoreType.DMA((3,)),
            pltpu.SemaphoreType.DMA((3, wins)),
            pltpu.SemaphoreType.DMA((3,)),
            pltpu.SemaphoreType.DMA((2,)),
            pltpu.SemaphoreType.REGULAR((2,)),
        ],
        compiler_params=pltpu.CompilerParams(
            collective_id=0, has_side_effects=True, vmem_limit_bytes=48 * 1024 * 1024
        ),
        name="correlate",
    )(*(pltpu.with_memory_space_constraint(operand, pltpu.HBM) for operand in operands), pair_count.reshape(1, 1))
    return out.reshape(LAGS // wins, 4, CH)


def solution(mesh):
    chips, wins = mesh.shape["pair"] // 2, mesh.shape["win"]
    placed = (P("win", None, "pair"), P("pair", None), P("pair"), P("pair", None))
    return jax.shard_map(
        functools.partial(local, chips, wins),
        mesh=mesh,
        in_specs=placed,
        out_specs=P("win", "pair", None),
        check_vma=False,
    )
```

```python
import functools
import math

import jax
import jax.numpy as jnp
import numpy as np
from jax import lax
from jax.experimental import pallas as pl
from jax.experimental.pallas import tpu as pltpu
from jax.sharding import PartitionSpec as P

FB = 512
F0 = 64
LAGS = 512
LENGTH = 2048
CH = 128
SPLIT = 4
FOLD = LENGTH // SPLIT
QUARTERS = 4
HALVES = 1
ROWS = 8
SEND = jnp.bfloat16
MESH = pl.DeviceIdType.MESH
ROW = 8
OWN_PAIRS = ((2, 3), (2, 4), (2, 5), (3, 4), (3, 5))
BEFORE_PAIRS = ((0, 4), (1, 4), (1, 5))
BEYOND_PAIRS = ((2, 6), (3, 6), (3, 7))
COUNT = 12
TILES = ((0, 1), (2, 2), (3, 4), (5, 5), (6, 7), (8, 8), (9, 10))


def quarter_bins(quarter):
    steps = 8 * np.arange(FB // 8)
    return np.concatenate([steps + 2 * quarter, steps + 2 * quarter + 1])


def two_parts(table):
    high = table.astype(jnp.bfloat16)
    rest = (table - high.astype(np.float64)).astype(jnp.bfloat16)
    return high, rest


def forward_table():
    nfft = 2 * LENGTH
    parts = []
    for quarter in range(QUARTERS):
        phase = 2 * np.pi * ((F0 + quarter_bins(quarter))[:, None] * np.arange(FOLD)[None, :] % nfft) / nfft
        table = np.concatenate([np.cos(phase), -np.sin(phase)], axis=0)
        parts.append(table)
    return np.stack(two_parts(np.concatenate(parts, axis=0)))


def lag_turns():
    bins = np.concatenate([quarter_bins(quarter) for quarter in range(QUARTERS)])
    phase = 2 * np.pi * ((F0 + bins) * (LAGS // 2) % (2 * LENGTH)) / (2 * LENGTH)
    return np.stack([np.cos(phase), np.sin(phase)]).astype(np.float32)


def weighted(terms):
    total = None
    for weight, value in terms:
        if abs(weight) < 1e-9:
            continue
        if abs(abs(weight) - 1.0) > 1e-9:
            value = value * np.float32(abs(weight))
        if total is None:
            total = value if weight > 0 else -value
        else:
            total = total + value if weight > 0 else total - value
    return total


def kernel(
    chips, wins, factor, x_hbm, fwd_hbm, turn_hbm, off_hbm, mask_hbm, cnt_ref, out_ref,
    xbuf, fwd, turn_ref, off_ref, mask_ref, spec, gath, acc, res, fin,
    load_sem, a_send, a_recv, z_send, z_recv, f_send, f_recv, ready,
):
    pair, win = lax.axis_index("pair"), lax.axis_index("win")
    chip, core = pair // 2, pair % 2
    place = chip % ROW
    low = place == 0
    high = (place == ROW - 1) | (chip == chips - 1)
    has_before, has_after = chip > 0, chip < chips - 1
    group = win * 2 + core
    groups = 2 * wins
    tiles = len(TILES)

    def device(chip_shift, side, there):
        return (2 * (chip + chip_shift) + side, there)

    x_copy = pltpu.make_async_copy(x_hbm.at[0], xbuf, load_sem.at[0])
    x_copy.start()
    fwd_copies = []
    for part in range(2):
        for side in range(2):
            rows = pl.ds(side * FB, FB)
            copy = pltpu.make_async_copy(fwd_hbm.at[part, rows], fwd.at[part, rows], load_sem.at[1 + len(fwd_copies)])
            copy.start()
            fwd_copies.append(copy)
    small_copies = []
    for source, target in ((turn_hbm, turn_ref), (off_hbm, off_ref), (mask_hbm, mask_ref)):
        copy = pltpu.make_async_copy(source, target, load_sem.at[1 + QUARTERS + len(small_copies)])
        copy.start()
        small_copies.append(copy)

    barrier = pltpu.get_barrier_semaphore()

    def near(step):
        turn = (step % 2) * ((step + 1) // 2) + (1 - step % 2) * (wins - step // 2)
        return (win + turn) % wins

    def greet(step, carry):
        there, side = near(wins - 1 - step // 2), (core + 1 + step % 2) % 2
        pl.semaphore_signal(barrier, inc=1, device_id=device(0, side, there), device_id_type=MESH)
        return carry

    lax.fori_loop(0, groups - 1, greet, 0)

    @pl.when(jnp.logical_not(high))
    def _():
        def greet_after(step, carry):
            there = near(wins - 1 - step // 2)
            pl.semaphore_signal(barrier, inc=1, device_id=device(1, step % 2, there), device_id_type=MESH)
            return carry

        lax.fori_loop(0, groups, greet_after, 0)

    @pl.when(low & has_before)
    def _():
        pl.semaphore_signal(barrier, inc=1, device_id=device(-1, core, win), device_id_type=MESH)

    acc[...] = jnp.zeros_like(acc)

    @pl.when(jnp.logical_not(has_after))
    def _():
        gath[2:4] = jnp.zeros_like(gath[2:4])

    def exchange(half, there, side):
        return pltpu.make_async_remote_copy(
            src_ref=spec.at[half, there * 2 + side],
            dst_ref=gath.at[1, win, core, half],
            send_sem=a_send,
            recv_sem=a_recv.at[win],
            device_id=device(0, side, there),
            device_id_type=MESH,
        )

    def settle(ref, sem):
        pltpu.make_async_copy(ref, ref, sem).wait()

    x_copy.wait()
    wide = jnp.concatenate([xbuf[h * FOLD:(h + 1) * FOLD, :] for h in range(SPLIT)], axis=1)
    wholes = []
    for part in range(2):
        for side in range(2):
            fwd_copies[2 * part + side].wait()
            product = jnp.dot(fwd[part, side * FB:(side + 1) * FB], wide, preferred_element_type=jnp.float32)
            if part == 0:
                wholes.append(product)
            else:
                wholes[side] += product
    for half in range(HALVES):
        for part in range(QUARTERS // HALVES):
            quarter = half * (QUARTERS // HALVES) + part
            whole = wholes[quarter // 2][quarter % 2 * 256:quarter % 2 * 256 + 256]
            reals, imags = [], []
            for odd in range(2):
                residue = 2 * quarter + odd
                real_terms, imag_terms = [], []
                for h in range(SPLIT):
                    turn = 2 * math.pi * ((residue * h) % 8) / 8
                    real = whole[odd * 64:odd * 64 + 64, h * CH:(h + 1) * CH]
                    imag = whole[128 + odd * 64:128 + odd * 64 + 64, h * CH:(h + 1) * CH]
                    real_terms += [(math.cos(turn), real), (math.sin(turn), imag)]
                    imag_terms += [(math.cos(turn), imag), (-math.sin(turn), real)]
                reals.append(weighted(real_terms))
                imags.append(weighted(imag_terms))
            for kind, value in enumerate((reals, imags)):
                turned = jnp.concatenate(value, axis=0).T.reshape(groups, ROWS, 128)
                lane = part * 256 + kind * 128
                spec[half, :, :, lane:lane + 128] = turned.astype(jnp.bfloat16)
        if half == 0:
            later = jnp.where(high & has_after, 1, 0)
            pl.semaphore_wait(barrier, groups - 1 + jnp.where(low, 0, groups) + later)

            @pl.when(jnp.logical_not(low))
            def _():
                pl.semaphore_signal(ready.at[0], inc=1, device_id=device(-1, core, win), device_id_type=MESH)

            @pl.when(high & has_after)
            def _():
                pl.semaphore_signal(ready.at[1], inc=1, device_id=device(1, core, win), device_id_type=MESH)

        def send(step, carry, half=half):
            exchange(half, near(step // 2), (core + step % 2) % 2).start()
            return carry

        lax.fori_loop(1, groups, send, 0)
        gath[1, win, core, half] = spec[half, group]

    def forward(there, kind):
        return pltpu.make_async_remote_copy(
            src_ref=gath.at[(1, 1, 2)[kind], there],
            dst_ref=gath.at[(0, 2, 3)[kind], there],
            send_sem=z_send.at[kind],
            recv_sem=z_recv.at[kind, there],
            device_id=device((1, -1, -1)[kind], core, win),
            device_id_type=MESH,
        )

    def multiply(there, pairs, base):
        used = sorted({block for both in pairs for block in both})
        for quarter in range(QUARTERS):
            half, lane = quarter // (QUARTERS // HALVES), quarter % (QUARTERS // HALVES) * 256
            blocks = {}
            for block in used:
                both = gath[block // 2, there, block % 2, half, :, lane:lane + 256].astype(jnp.float32)
                blocks[block] = (both[:, :128], both[:, 128:])
            for index, (own, other) in enumerate(pairs):
                (own_real, own_imag), (other_real, other_imag) = blocks[own], blocks[other]
                rows = slice((base + index) * ROWS, (base + index + 1) * ROWS)
                left = slice(quarter * 256, quarter * 256 + 128)
                right = slice(quarter * 256 + 128, quarter * 256 + 256)
                acc[rows, left] += own_real * other_real + own_imag * other_imag
                acc[rows, right] += own_imag * other_real - own_real * other_imag

    lag = 6

    def travel(step, carry):
        @pl.when(step < wins)
        def _():
            there = near(step)

            @pl.when(step == 0)
            def _():
                settle(gath.at[1, win, 1 - core], a_recv.at[win])

            @pl.when(step > 0)
            def _():
                settle(gath.at[1, there], a_recv.at[there])

            @pl.when(jnp.logical_not(high))
            def _():
                @pl.when(step == 0)
                def _():
                    pl.semaphore_wait(ready.at[0], 1)

                forward(there, 0).start()

            @pl.when(has_before)
            def _():
                @pl.when(low & (step == 0))
                def _():
                    pl.semaphore_wait(ready.at[1], 1)

                forward(there, 1).start()

        @pl.when(step >= lag)
        def _():
            there = near(step - lag)

            @pl.when(has_after)
            def _():
                forward(there, 1).wait_recv()

            @pl.when(low & has_before)
            def _():
                forward(there, 2).start()

            multiply(there, OWN_PAIRS, 0)

            @pl.when(jnp.logical_not(low))
            def _():
                forward(there, 0).wait_recv()
                multiply(there, BEFORE_PAIRS, len(OWN_PAIRS))

            @pl.when(high & has_after)
            def _():
                forward(there, 2).wait_recv()
                multiply(there, BEYOND_PAIRS, len(OWN_PAIRS) + len(BEFORE_PAIRS))
        return carry

    lax.fori_loop(0, wins + lag, travel, 0)

    for copy in small_copies:
        copy.wait()
    count = COUNT * ROWS
    stacks = jnp.zeros((count, LAGS), jnp.float32)
    for quarter in range(QUARTERS):
        bins = slice(quarter * 128, quarter * 128 + 128)
        cosine, sine = turn_ref[0:1, bins] * factor, turn_ref[1:2, bins] * factor
        real = acc[:, quarter * 256:quarter * 256 + 128]
        imag = acc[:, quarter * 256 + 128:quarter * 256 + 256]
        cross = jnp.concatenate([real * cosine + imag * sine, imag * cosine - real * sine], axis=1)
        high_part = cross.astype(jnp.bfloat16)
        rest = (cross - high_part.astype(jnp.float32)).astype(jnp.bfloat16)
        both = jnp.concatenate([high_part, rest], axis=0)
        upper = jnp.dot(both, fwd[0, quarter * 256:quarter * 256 + 256], preferred_element_type=jnp.float32)
        stacks += upper[:count] + upper[count:]
        stacks += jnp.dot(high_part, fwd[1, quarter * 256:quarter * 256 + 256], preferred_element_type=jnp.float32)
    lanes = lax.broadcasted_iota(jnp.int32, (ROWS, 128), 1)
    for column in range(LAGS // 128):
        for tile, (left, right) in enumerate(TILES):
            a = stacks[left * ROWS:(left + 1) * ROWS, column * 128:(column + 1) * 128]
            b = stacks[right * ROWS:(right + 1) * ROWS, column * 128:(column + 1) * 128]
            even = jnp.where(lanes < 64, a, pltpu.roll(b, 64, 1))
            odd = jnp.where(lanes < 64, pltpu.roll(a, 64, 1), b)
            res[2 * column * tiles + tile] = even.astype(SEND)
            res[(2 * column + 1) * tiles + tile] = odd.astype(SEND)

    def deliver(there, kind):
        first, size, slot = ((0, 2, 0), (2, 1, 0), (3, 1, 2), (4, 1, 2), (5, 1, 2), (6, 1, 2))[kind]
        return pltpu.make_async_remote_copy(
            src_ref=res.at[pl.ds(there * tiles + first, size)],
            dst_ref=fin.at[group, slot:slot + size],
            send_sem=f_send.at[kind // 2],
            recv_sem=f_recv.at[0 if kind < 2 else 1],
            device_id=device(-1 if kind // 2 == 1 else 0, kind % 2, there),
            device_id_type=MESH,
        )

    def hand_out(step, carry):
        there = near(wins - 1 - step)

        @pl.when(jnp.logical_not(low))
        def _():
            deliver(there, 2).start()
            deliver(there, 3).start()

        for side in range(2):
            @pl.when((step < wins - 1) | (core != side))
            def _():
                deliver(there, side).start()

                @pl.when(high)
                def _():
                    deliver(there, 4 + side).start()
        return carry

    lax.fori_loop(0, wins, hand_out, 0)
    mine = win * tiles

    @pl.when(core == 0)
    def _():
        fin[group, 0:2] = res[pl.ds(mine, 2)]

    @pl.when(core == 1)
    def _():
        fin[group, 0:1] = res[pl.ds(mine + 2, 1)]

    @pl.when(high)
    def _():
        fin[group, 2:3] = res[pl.ds(mine + 5 + core, 1)]

    settle(spec.at[:, 0:groups - 1], a_send)

    @pl.when(jnp.logical_not(high))
    def _():
        settle(gath.at[1], z_send.at[0])

    @pl.when(has_before)
    def _():
        settle(gath.at[1], z_send.at[1])

    @pl.when(low & has_before)
    def _():
        settle(gath.at[1], z_send.at[2])

    @pl.when(core == 0)
    def _():
        settle(fin.at[0:groups - 1, 0:2], f_recv.at[0])

    @pl.when(core == 1)
    def _():
        settle(fin.at[0:groups - 1, 0:1], f_recv.at[0])

    first = fin[:, 0].astype(jnp.float32).reshape(CH, 128).T
    third = fin[:, 1].astype(jnp.float32).reshape(CH, 128)

    @pl.when(high)
    def _():
        settle(fin.at[0:groups - 1, 2:3], f_recv.at[1])

    @pl.when(jnp.logical_not(high))
    def _():
        settle(fin.at[:, 2:3], f_recv.at[1])

    last = fin[:, 2].astype(jnp.float32).reshape(CH, 128)
    wide_lanes = lax.broadcasted_iota(jnp.int32, (CH, 128), 1)
    second = jnp.where((wide_lanes < 64) & (core == 0), third, last)
    second = second.T
    choices = (first[:64], first[64:], second[:64], second[64:])
    for slot in range(4):
        offset = off_ref[0, slot]
        picked = choices[3]
        for index in range(3):
            picked = jnp.where(offset == index + 1, choices[index], picked)
        weight = mask_ref[slot:slot + 1, :].astype(jnp.float32)
        picked = jnp.where(slot < cnt_ref[0, 0], picked * weight, 0.0)
        out_ref[pl.ds(slot, 64, stride=4), :] = picked

    @pl.when(core == 0)
    def _():
        settle(res.at[0:3 * wins - 2], f_send.at[0])

    @pl.when(core == 1)
    def _():
        settle(res.at[0:3 * wins - 1], f_send.at[0])

    @pl.when(jnp.logical_not(low))
    def _():
        settle(res.at[0:groups], f_send.at[1])

    @pl.when(high)
    def _():
        settle(res.at[0:groups - 1], f_send.at[2])


def local(chips, wins, windows, pair_offset, pair_count, pair_mask):
    groups = 2 * wins
    fwd_table = jnp.asarray(forward_table())
    factor = 1.0 / (LENGTH * math.sqrt(FB * windows.shape[0] * wins))
    hbm = pl.BlockSpec(memory_space=pltpu.HBM)
    operands = (windows, fwd_table, jnp.asarray(lag_turns()), pair_offset, pair_mask)
    vmem = pl.BlockSpec(memory_space=pltpu.VMEM)
    out = pl.pallas_call(
        functools.partial(kernel, chips, wins, factor),
        out_shape=jax.ShapeDtypeStruct((LAGS // wins * 4, CH), jnp.float32),
        in_specs=[hbm] * len(operands) + [pl.BlockSpec(memory_space=pltpu.SMEM)],
        out_specs=vmem,
        scratch_shapes=[
            pltpu.VMEM((LENGTH, CH), jnp.bfloat16),
            pltpu.VMEM(fwd_table.shape, jnp.bfloat16),
            pltpu.VMEM((2, FB), jnp.float32),
            pltpu.SMEM(pair_offset.shape, jnp.int32),
            pltpu.VMEM(pair_mask.shape, jnp.int32),
            pltpu.VMEM((HALVES, groups, ROWS, 2 * FB // HALVES), jnp.bfloat16),
            pltpu.VMEM((4, wins, 2, HALVES, ROWS, 2 * FB // HALVES), jnp.bfloat16),
            pltpu.VMEM((COUNT * ROWS, 2 * FB), jnp.float32),
            pltpu.VMEM((wins * len(TILES), ROWS, 128), SEND),
            pltpu.VMEM((groups, 3, ROWS, 128), SEND),
            pltpu.SemaphoreType.DMA((4 + QUARTERS,)),
            pltpu.SemaphoreType.DMA,
            pltpu.SemaphoreType.DMA((wins,)),
            pltpu.SemaphoreType.DMA((3,)),
            pltpu.SemaphoreType.DMA((3, wins)),
            pltpu.SemaphoreType.DMA((3,)),
            pltpu.SemaphoreType.DMA((2,)),
            pltpu.SemaphoreType.REGULAR((2,)),
        ],
        compiler_params=pltpu.CompilerParams(
            collective_id=0, has_side_effects=True, vmem_limit_bytes=48 * 1024 * 1024
        ),
        name="correlate",
    )(*(pltpu.with_memory_space_constraint(operand, pltpu.HBM) for operand in operands), pair_count.reshape(1, 1))
    return out.reshape(LAGS // wins, 4, CH)


def solution(mesh):
    chips, wins = mesh.shape["pair"] // 2, mesh.shape["win"]
    placed = (P("win", None, "pair"), P("pair", None), P("pair"), P("pair", None))
    return jax.shard_map(
        functools.partial(local, chips, wins),
        mesh=mesh,
        in_specs=placed,
        out_specs=P("win", "pair", None),
        check_vma=False,
    )
```
